128 devices in a mesh: group: 4 (over y_hi, core), blk: 32 (over y_lo, z, x).
Axes of the slice: x: 4, y: 4 (y_hi: 2, y_lo: 2; y = y_hi * 2 + y_lo), z: 4, core: 2. Of those that a mesh axis runs over, the one named last changes fastest.
Arguments:
- points: bfloat16 [1048576, 768], P(('group', 'blk')), may hold values from -128 to 128
- block_lists: int32 [8192, 4], P(('group', 'blk')), may hold values from 0 to 511, as said below
- centroids: bfloat16 [32768, 768], P('blk'), may hold values from -6 to 6
- dual_weights: bfloat16 [32768], P('blk'), may hold values from -1 to 1
Outputs:
- new_centroids: bfloat16 [32768, 768], P('blk')
- new_weights: bfloat16 [32768], P('blk')
The draws below stay inside these ranges and needn't reach their ends.
Inputs may be any that keep to these rules, and one draw needn't show every extreme that they name: `block_lists`: cycle position q (index q along blk) owns blocks q * 16 to (q + 1) * 16 - 1. For a tile held by a device at cycle position p, slot 0 names a block of position p - 1, slot 2 a block of position p + 1, and slots 1 and 3 two different blocks of position p, positions taken modulo the number of devices along blk.
All inputs are finite; a program needn't handle non-finite values.
Results may differ from the reference program's by a relative error of at most 0.0052.
Values may be sent and summed in bfloat16 or wider, within the bound.
A program may use at most 128 MiB of HBM per device.

```python
import math
import jax
import jax.numpy as jnp
from jax import lax

D = 768
BLOCK = 64
TILE = 128
SLOTS = 4
ITERS = 2
CB_DEV = 16
P_DEV = 8192
K = 32768
POINTS = 1048576


def drawn_lists(key):
    tile_count = POINTS // TILE
    cycle_size = K // (CB_DEV * BLOCK)
    tile_index = jnp.arange(tile_count, dtype=jnp.int32)
    position = tile_index // (P_DEV // TILE) % cycle_size
    keys = jax.random.split(jax.random.fold_in(key, 21), 4)
    lower = jax.random.randint(keys[0], (tile_count,), 0, CB_DEV, dtype=jnp.int32)
    upper = jax.random.randint(keys[1], (tile_count,), 0, CB_DEV, dtype=jnp.int32)
    own_first = jax.random.randint(keys[2], (tile_count,), 0, CB_DEV, dtype=jnp.int32)
    own_step = jax.random.randint(keys[3], (tile_count,), 1, CB_DEV, dtype=jnp.int32)
    left_block = (position - 1) % cycle_size * CB_DEV + lower
    right_block = (position + 1) % cycle_size * CB_DEV + upper
    own_one = position * CB_DEV + own_first
    own_two = position * CB_DEV + (own_first + own_step) % CB_DEV
    return jnp.stack([left_block, own_one, right_block, own_two], axis=-1).astype(jnp.int32)


def drawn_centroids(key):
    values = jnp.clip(jax.random.normal(jax.random.fold_in(key, 22), (K, D), jnp.float32), -6.0, 6.0)
    return values.astype(jnp.bfloat16).astype(jnp.float32)


def drawn_weights(key):
    values = jax.random.uniform(jax.random.fold_in(key, 23), (K,), jnp.float32, -1.0, 1.0)
    return values.astype(jnp.bfloat16).astype(jnp.float32)


def draw_block_lists(key, part):
    return drawn_lists(key).astype(jnp.int32)


def draw_centroids(key, part):
    return drawn_centroids(key).astype(jnp.bfloat16)


def draw_dual_weights(key, part):
    return drawn_weights(key).astype(jnp.bfloat16)


def draw_points(key, part):
    keys = jax.random.split(jax.random.fold_in(key, 24), 1)
    values = jnp.clip(jax.random.normal(keys[0], (POINTS, D), jnp.float32), -6.0, 6.0)
    values = jnp.clip(values, -128.0, 128.0)
    return values.astype(jnp.bfloat16)


def setup_inputs(seed: int = 0) -> dict:
    splits = jax.random.split(jax.random.key(seed), 5)
    return {
        "points": draw_points(jax.random.fold_in(splits[4], 71), 0),
        "block_lists": draw_block_lists(jax.random.fold_in(splits[4], 71), 0),
        "centroids": draw_centroids(jax.random.fold_in(splits[4], 71), 0),
        "dual_weights": draw_dual_weights(jax.random.fold_in(splits[4], 71), 0),
    }


prior_mass = 1.0
dual_step = 0.5


def assign_pass(points, block_lists, centroids, weights):
    block_count = K // BLOCK
    base = centroids.astype(jnp.float32)
    offsets = weights.astype(jnp.float32) - jnp.sum(base * base, axis=1) * (16.0 / D)
    cand_blocks = base.reshape(block_count, BLOCK, D)
    offset_blocks = offsets.reshape(block_count, BLOCK)
    tile_count = block_lists.shape[0]
    group_size = math.gcd(tile_count, 64)
    tiled_points = points.reshape(tile_count // group_size, group_size, TILE, D)
    tiled_ids = block_lists.reshape(tile_count // group_size, group_size, SLOTS)

    def tile_step(running, packet):
        sum_num, sum_mass = running
        tile_points, block_ids = packet
        point_vals = tile_points.astype(jnp.float32)
        candidates = cand_blocks[block_ids].reshape(group_size, SLOTS * BLOCK, D)
        scores = jnp.einsum("tpd,tkd->tpk", point_vals, candidates) * (32.0 / D)
        scores = scores + offset_blocks[block_ids].reshape(group_size, 1, SLOTS * BLOCK)
        membership = lax.optimization_barrier(jax.nn.softmax(scores, axis=-1).astype(jnp.bfloat16)).astype(jnp.float32)
        masses = jnp.sum(membership, axis=1).reshape(group_size * SLOTS, BLOCK)
        numerator = jnp.einsum("tpk,tpd->tkd", membership, point_vals).reshape(group_size * SLOTS, BLOCK, D)
        flat_ids = block_ids.reshape(-1)
        return (sum_num.at[flat_ids].add(numerator), sum_mass.at[flat_ids].add(masses)), None

    start = (jnp.zeros((block_count, BLOCK, D), jnp.float32), jnp.zeros((block_count, BLOCK), jnp.float32))
    (sum_num, sum_mass), _ = lax.scan(tile_step, start, (tiled_points, tiled_ids))
    return sum_num.reshape(K, D), sum_mass.reshape(K)


def reference(points, block_lists, centroids, dual_weights):
    target = POINTS / K
    weights = dual_weights
    for sweep in range(ITERS):
        totals_num, totals_mass = assign_pass(points, block_lists, centroids, weights)
        base = centroids.astype(jnp.float32)
        centroids = ((totals_num + prior_mass * base) / (totals_mass + prior_mass)[:, None]).astype(jnp.bfloat16)
        weights = (weights.astype(jnp.float32) + dual_step * (1.0 - totals_mass / target)).astype(jnp.bfloat16)
    return centroids, weights
```

```python
import functools

import jax
import jax.numpy as jnp
from jax import lax
from jax.experimental import pallas as pl
from jax.experimental.pallas import tpu as pltpu
from jax.sharding import PartitionSpec as P

D = 768
BLOCK = 64
TILE = 128
SLOTS = 4
ITERS = 2


prior_mass = 1.0
dual_step = 0.5


def passed_along(block, axis, distance):
    devices = range(lax.axis_size(axis))
    route = [((i - distance) % len(devices), i) for i in devices]
    return lax.ppermute(block, axis, route)


def with_halo(cells, sides, width):
    for axis, dim in sides:
        count = lax.axis_size(axis)
        head = lax.slice_in_dim(cells, 0, width, axis=dim)
        tail = lax.slice_in_dim(cells, cells.shape[dim] - width, cells.shape[dim], axis=dim)
        cells = jnp.concatenate(
            [
                lax.ppermute(tail, axis, [(i, (i + 1) % count) for i in range(count)]),
                cells,
                lax.ppermute(head, axis, [((i + 1) % count, i) for i in range(count)]),
            ],
            axis=dim,
        )
    return cells


def renew_blocks(numerator, masses, centroids, weights, target):
    base = centroids.astype(jnp.float32)
    fresh = ((numerator + prior_mass * base) / (masses + prior_mass)[:, None]).astype(jnp.bfloat16)
    renewed = (weights.astype(jnp.float32) + dual_step * (1.0 - masses / target)).astype(
        jnp.bfloat16
    )
    return (fresh, renewed)


def return_cycle(near_num, near_mass):
    upper_num, upper_mass = passed_along((near_num[0], near_mass[0]), "blk", -1)
    lower_num, lower_mass = passed_along((near_num[2], near_mass[2]), "blk", 1)
    return (near_num[1] + upper_num + lower_num, near_mass[1] + upper_mass + lower_mass)


def tile_kernel(ids_ref, pts_ref, cand_ref, off_ref, num_ref, mass_ref):
    t = pl.program_id(0)

    @pl.when(t == 0)
    def _():
        num_ref[...] = jnp.zeros_like(num_ref)
        mass_ref[...] = jnp.zeros_like(mass_ref)

    x = pts_ref[...]
    ids = [ids_ref[t, s] for s in range(SLOTS)]
    cands = jnp.concatenate([cand_ref[i] for i in ids], axis=0)
    offs = jnp.concatenate([off_ref[i] for i in ids], axis=1)
    scores = lax.dot_general(
        x, cands, (((1,), (1,)), ((), ())), preferred_element_type=jnp.float32
    ) * (32.0 / D)
    scores = scores + offs
    top = jnp.max(scores, axis=-1, keepdims=True)
    unnorm = jnp.exp(scores - top)
    member = (unnorm / jnp.sum(unnorm, axis=-1, keepdims=True)).astype(jnp.bfloat16)
    mass = jnp.sum(member.astype(jnp.float32), axis=0, keepdims=True)
    num = lax.dot_general(
        member, x, (((0,), (0,)), ((), ())), preferred_element_type=jnp.float32
    )
    for s in range(SLOTS):
        i = ids[s]
        num_ref[i] += num[s * BLOCK:(s + 1) * BLOCK]
        mass_ref[i] += mass[:, s * BLOCK:(s + 1) * BLOCK]


def assign_tiles(points, near_ids, near_centroids, offsets):
    tile_count = near_ids.shape[0]
    width = points.shape[1]
    block_total = near_centroids.shape[0] // BLOCK
    cand = near_centroids.reshape(block_total, BLOCK, width)
    off = offsets.reshape(block_total, 1, BLOCK)
    flops = 4 * tile_count * TILE * SLOTS * BLOCK * width
    num, mass = pl.pallas_call(
        tile_kernel,
        out_shape=(
            jax.ShapeDtypeStruct((block_total, BLOCK, width), jnp.float32),
            jax.ShapeDtypeStruct((block_total, 1, BLOCK), jnp.float32),
        ),
        grid_spec=pltpu.PrefetchScalarGridSpec(
            num_scalar_prefetch=1,
            grid=(tile_count,),
            in_specs=[
                pl.BlockSpec((TILE, width), lambda t, ids: (t, 0)),
                pl.BlockSpec((block_total, BLOCK, width), lambda t, ids: (0, 0, 0)),
                pl.BlockSpec((block_total, 1, BLOCK), lambda t, ids: (0, 0, 0)),
            ],
            out_specs=[
                pl.BlockSpec((block_total, BLOCK, width), lambda t, ids: (0, 0, 0)),
                pl.BlockSpec((block_total, 1, BLOCK), lambda t, ids: (0, 0, 0)),
            ],
        ),
        compiler_params=pltpu.CompilerParams(
            dimension_semantics=("arbitrary",), vmem_limit_bytes=56 * 1024 * 1024
        ),
        cost_estimate=pl.CostEstimate(
            flops=flops,
            transcendentals=tile_count * TILE * SLOTS * BLOCK,
            bytes_accessed=points.size * 2 + cand.size * 2 + block_total * BLOCK * width * 4,
        ),
    )(near_ids, points, cand, off)
    return (num.reshape(3, -1, width), mass.reshape(3, -1))


def per_device(points, block_lists, centroids, dual_weights):
    own_rows = centroids.shape[0]
    own_blocks = own_rows // BLOCK
    cycle_size = lax.axis_size("blk")
    position = lax.axis_index("blk")
    groups = lax.axis_size("group")
    target = points.shape[0] * groups / own_rows
    owner = block_lists // own_blocks
    near_ids = (owner - position + 1) % cycle_size * own_blocks + block_lists % own_blocks
    weights = dual_weights
    for sweep in range(ITERS):
        near_centroids, near_weights = (
            with_halo(centroids, (("blk", 0),), own_rows),
            with_halo(weights, (("blk", 0),), own_rows),
        )
        squares = jnp.sum(jnp.square(near_centroids.astype(jnp.float32)), axis=1)
        offsets = near_weights.astype(jnp.float32) - squares * (16.0 / D)
        near_num, near_mass = assign_tiles(points, near_ids, near_centroids, offsets)
        own_num, own_mass = return_cycle(near_num, near_mass)
        total_num, total_mass = lax.psum((own_num, own_mass), "group")
        centroids, weights = renew_blocks(total_num, total_mass, centroids, weights, target)
    return (centroids, weights)


def solution(mesh):
    return jax.shard_map(
        per_device,
        mesh=mesh,
        in_specs=(P(("group", "blk"), None), P(("group", "blk"), None), P("blk", None), P("blk")),
        out_specs=(P("blk", None), P("blk")),
        check_vma=False,
    )
```

```python
import functools

import jax
import jax.numpy as jnp
from jax import lax
from jax.experimental import pallas as pl
from jax.experimental.pallas import tpu as pltpu
from jax.sharding import PartitionSpec as P

D = 768
BLOCK = 64
TILE = 128
SLOTS = 4
ITERS = 2


prior_mass = 1.0
dual_step = 0.5


def passed_along(block, axis, distance):
    devices = range(lax.axis_size(axis))
    route = [((i - distance) % len(devices), i) for i in devices]
    return lax.ppermute(block, axis, route)


def with_halo(cells, sides, width):
    for axis, dim in sides:
        count = lax.axis_size(axis)
        head = lax.slice_in_dim(cells, 0, width, axis=dim)
        tail = lax.slice_in_dim(cells, cells.shape[dim] - width, cells.shape[dim], axis=dim)
        cells = jnp.concatenate(
            [
                lax.ppermute(tail, axis, [(i, (i + 1) % count) for i in range(count)]),
                cells,
                lax.ppermute(head, axis, [((i + 1) % count, i) for i in range(count)]),
            ],
            axis=dim,
        )
    return cells


def renew_blocks(numerator, masses, centroids, weights, target):
    base = centroids.astype(jnp.float32)
    fresh = ((numerator + prior_mass * base) / (masses + prior_mass)[:, None]).astype(jnp.bfloat16)
    renewed = (weights.astype(jnp.float32) + dual_step * (1.0 - masses / target)).astype(
        jnp.bfloat16
    )
    return (fresh, renewed)


def return_cycle(near_num, near_mass):
    upper_num, upper_mass = passed_along((near_num[0], near_mass[0]), "blk", -1)
    lower_num, lower_mass = passed_along((near_num[2], near_mass[2]), "blk", 1)
    return (near_num[1] + upper_num + lower_num, near_mass[1] + upper_mass + lower_mass)


def tile_kernel(per_step, ids_ref, pts_ref, cand_ref, off_ref, num_ref, mass_ref):
    t = pl.program_id(0)

    @pl.when(t == 0)
    def _():
        num_ref[...] = jnp.zeros_like(num_ref)
        mass_ref[...] = jnp.zeros_like(mass_ref)

    for k in range(per_step):
        tile = t * per_step + k
        x = pts_ref[k * TILE:(k + 1) * TILE, :]
        ids = [ids_ref[tile, s] for s in range(SLOTS)]
        cands = jnp.concatenate([cand_ref[i] for i in ids], axis=0)
        offs = jnp.concatenate([off_ref[i] for i in ids], axis=1)
        scores = lax.dot_general(
            x, cands, (((1,), (1,)), ((), ())), preferred_element_type=jnp.float32
        ) * (32.0 / D)
        scores = scores + offs
        top = jnp.max(scores, axis=-1, keepdims=True)
        unnorm = jnp.exp(scores - top)
        member = (unnorm / jnp.sum(unnorm, axis=-1, keepdims=True)).astype(jnp.bfloat16)
        mass = jnp.sum(member.astype(jnp.float32), axis=0, keepdims=True)
        num = lax.dot_general(
            member, x, (((0,), (0,)), ((), ())), preferred_element_type=jnp.float32
        )
        for s in range(SLOTS):
            i = ids[s]
            num_ref[i] += num[s * BLOCK:(s + 1) * BLOCK]
            mass_ref[i] += mass[:, s * BLOCK:(s + 1) * BLOCK]


PER_STEP = 8


def assign_tiles(points, near_ids, near_centroids, offsets):
    tile_count = near_ids.shape[0]
    width = points.shape[1]
    block_total = near_centroids.shape[0] // BLOCK
    cand = near_centroids.reshape(block_total, BLOCK, width)
    off = offsets.reshape(block_total, 1, BLOCK)
    flops = 4 * tile_count * TILE * SLOTS * BLOCK * width
    num, mass = pl.pallas_call(
        functools.partial(tile_kernel, PER_STEP),
        out_shape=(
            jax.ShapeDtypeStruct((block_total, BLOCK, width), jnp.float32),
            jax.ShapeDtypeStruct((block_total, 1, BLOCK), jnp.float32),
        ),
        grid_spec=pltpu.PrefetchScalarGridSpec(
            num_scalar_prefetch=1,
            grid=(tile_count // PER_STEP,),
            in_specs=[
                pl.BlockSpec((TILE * PER_STEP, width), lambda t, ids: (t, 0)),
                pl.BlockSpec((block_total, BLOCK, width), lambda t, ids: (0, 0, 0)),
                pl.BlockSpec((block_total, 1, BLOCK), lambda t, ids: (0, 0, 0)),
            ],
            out_specs=[
                pl.BlockSpec((block_total, BLOCK, width), lambda t, ids: (0, 0, 0)),
                pl.BlockSpec((block_total, 1, BLOCK), lambda t, ids: (0, 0, 0)),
            ],
        ),
        compiler_params=pltpu.CompilerParams(
            dimension_semantics=("arbitrary",), vmem_limit_bytes=56 * 1024 * 1024
        ),
        cost_estimate=pl.CostEstimate(
            flops=flops,
            transcendentals=tile_count * TILE * SLOTS * BLOCK,
            bytes_accessed=points.size * 2 + cand.size * 2 + block_total * BLOCK * width * 4,
        ),
    )(near_ids, points, cand, off)
    return (num.reshape(3, -1, width), mass.reshape(3, -1))


def per_device(points, block_lists, centroids, dual_weights):
    own_rows = centroids.shape[0]
    own_blocks = own_rows // BLOCK
    cycle_size = lax.axis_size("blk")
    position = lax.axis_index("blk")
    groups = lax.axis_size("group")
    target = points.shape[0] * groups / own_rows
    owner = block_lists // own_blocks
    near_ids = (owner - position + 1) % cycle_size * own_blocks + block_lists % own_blocks
    weights = dual_weights
    for sweep in range(ITERS):
        near_centroids, near_weights = (
            with_halo(centroids, (("blk", 0),), own_rows),
            with_halo(weights, (("blk", 0),), own_rows),
        )
        squares = jnp.sum(jnp.square(near_centroids.astype(jnp.float32)), axis=1)
        offsets = near_weights.astype(jnp.float32) - squares * (16.0 / D)
        near_num, near_mass = assign_tiles(points, near_ids, near_centroids, offsets)
        own_num, own_mass = return_cycle(near_num, near_mass)
        total_num, total_mass = lax.psum((own_num, own_mass), "group")
        centroids, weights = renew_blocks(total_num, total_mass, centroids, weights, target)
    return (centroids, weights)


def solution(mesh):
    return jax.shard_map(
        per_device,
        mesh=mesh,
        in_specs=(P(("group", "blk"), None), P(("group", "blk"), None), P("blk", None), P("blk")),
        out_specs=(P("blk", None), P("blk")),
        check_vma=False,
    )
```
